32 devices in a mesh: tm: 2 (over x), seq: 16 (over z, y, core).
Axes of the slice: x: 2, y: 2, z: 4, core: 2. Of those that a mesh axis runs over, the one named last changes fastest.
Arguments:
- tokens: bfloat16 [512, 5120], P(('tm', 'seq')), may hold values from -6 to 6
- w_query: bfloat16 [5120, 4096], P('seq'), may hold values from -0.078125 to 0.078125
- w_out: bfloat16 [4096, 5120], P(None, 'seq'), may hold values from -0.25 to 0.25
- k_cache: bfloat16 [4096, 4096], P(('tm', 'seq')), may hold values from -800 to 800
- v_cache: bfloat16 [4096, 4096], P(('tm', 'seq')), may hold values from -6 to 6
- radial_mask: int32 [16, 2, 32], replicated, may hold values from 0 to 1, as said below
- slot_frame: int32 [16], replicated, may hold values from 0 to 15, each once
Outputs:
- mixed: bfloat16 [512, 5120], P(('tm', 'seq'))
The draws below stay inside these ranges and needn't reach their ends.
Inputs may be any that keep to these rules, and one draw needn't show every extreme that they name: radial_mask[f, b, f * 2 + b] = 1 for every frame f and tile b. `slot_frame`: each of the 16 frames is held by exactly one slot.
All inputs are finite; a program needn't handle non-finite values.
Results may differ from the reference program's by a relative error of at most 0.012.
The reference program's roundings to bfloat16 on the way count: a program that leaves them out, or rounds other values in their place, can miss the bound.
Values may be sent and summed in bfloat16 or wider, within the bound.
A program may use at most 128 MiB of HBM per device.

```python
import jax
import jax.numpy as jnp
from jax import lax

D = 5120
HD = 128
HEADS = 32
FRAMES = 16
BLOCK = 128
HH = 4096
FT = 256
FB = 2
KEYS = 4096
N_TM = 2


def draw_k_cache(key, part):
    base = 2.5 * jnp.clip(jax.random.normal(jax.random.fold_in(key, 11), (KEYS, HEADS * HD), jnp.float32), -6.0, 6.0)
    return base.astype(jnp.bfloat16)


def draw_radial_mask(key, part):
    query_frame = jnp.arange(FRAMES, dtype=jnp.int32).reshape(FRAMES, 1, 1, 1)
    key_frame = jnp.arange(FRAMES, dtype=jnp.int32).reshape(1, 1, FRAMES, 1)
    query_block = jnp.arange(FB, dtype=jnp.int32).reshape(1, FB, 1, 1)
    key_block = jnp.arange(FB, dtype=jnp.int32).reshape(1, 1, 1, FB)
    distance = jnp.abs(query_frame - key_frame)
    band = jnp.zeros_like(distance)
    for level in range(1, 8):
        band = band + (distance + 1 >= 2 ** level).astype(jnp.int32)
    reach = jnp.maximum(jnp.right_shift(jnp.full_like(band, FB), band), 1)
    inside = jnp.abs(query_block - key_block) < reach
    kept = jax.random.randint(jax.random.fold_in(key, 21), (FRAMES, FB, FRAMES, FB), 0, 8) != 0
    diagonal = (distance == 0) & (query_block == key_block)
    mask = inside & kept | diagonal
    return mask.astype(jnp.int32).reshape(FRAMES, FB, FRAMES * FB)


def block_levels(stream_key, dims, pieces, least, largest):
    factor_of = 1.0
    for dim, shards_of in pieces:
        draws = jax.random.uniform(jax.random.fold_in(jax.random.fold_in(stream_key, 6), dim), (shards_of,), jnp.float32, least / len(pieces), largest / len(pieces))
        factor_of = factor_of * jnp.repeat(jnp.exp(draws), dims[dim] // shards_of).reshape((-1,) + (1,) * (len(dims) - 1 - dim))
    return factor_of


def gaussian(rng, shape, spread, bound, pieces=(), kind=jnp.bfloat16):
    drawn = spread * jax.random.normal(rng, shape, jnp.float32)
    if pieces:
        drawn = drawn * block_levels(rng, shape, pieces, -0.22, 0.18)
    return jnp.clip(drawn, -bound, bound).astype(kind)


def setup_inputs(seed: int = 0) -> dict:
    key_list = jax.random.split(jax.random.key(seed), 8)
    return {
        "tokens": gaussian(key_list[0], (N_TM * FT, D), 1.0, 6.0, ((0, 32),)),
        "w_query": gaussian(key_list[1], (D, HH), D ** -0.5, 0.078125, ((0, 16),)),
        "w_out": gaussian(key_list[2], (HH, D), (HH // 8) ** -0.5, 0.25, ((1, 16),)),
        "k_cache": draw_k_cache(jax.random.fold_in(key_list[7], 71), 0),
        "v_cache": gaussian(key_list[4], (KEYS, HH), 1.0, 6.0, ((0, 32),)),
        "radial_mask": draw_radial_mask(jax.random.fold_in(key_list[7], 71), 0),
        "slot_frame": jax.random.permutation(key_list[6], FRAMES).astype(jnp.int32),
    }


NEG = -1.0e30


def slot_allowed(radial_mask, slot_frame, frame):
    frame_blocks = radial_mask.shape[1]
    frames = slot_frame.shape[0]
    onehot = (slot_frame[:, None] == jnp.arange(frames, dtype=jnp.int32)[None, :]).astype(jnp.float32)
    chosen = lax.dynamic_index_in_dim(radial_mask, frame, 0, keepdims=False).astype(jnp.float32)
    chosen = chosen.reshape(frame_blocks, frames, frame_blocks)
    return jnp.einsum("sf,qfb->qsb", onehot, chosen).reshape(frame_blocks, frames * frame_blocks)


def reference(tokens, w_query, w_out, k_cache, v_cache, radial_mask, slot_frame):
    frame_tok = tokens.shape[0] // N_TM
    per_group = FRAMES // N_TM
    score_scale = HD ** -0.5
    key_heads = k_cache.reshape(-1, HEADS, HD).transpose(1, 0, 2)
    value_heads = v_cache.reshape(-1, HEADS, HD).transpose(1, 0, 2)
    results = []
    for group in range(N_TM):
        frame = slot_frame[group * per_group]
        allowed = slot_allowed(radial_mask, slot_frame, frame) > 0.5
        allowed = jnp.repeat(jnp.repeat(allowed, BLOCK, axis=0), BLOCK, axis=1)
        group_rows = tokens[group * frame_tok:(group + 1) * frame_tok]
        query = jnp.dot(group_rows, w_query, preferred_element_type=jnp.float32).astype(jnp.bfloat16)
        query_heads = query.reshape(frame_tok, HEADS, HD).transpose(1, 0, 2)

        def attend(operands):
            q_head, k_head, v_head = operands
            scores = jnp.dot(q_head, k_head.T, preferred_element_type=jnp.float32) * score_scale
            scores = jnp.where(allowed, scores, NEG)
            highest = jnp.max(scores, axis=1, keepdims=True)
            weights = jnp.where(allowed, jnp.exp(scores - highest), 0.0)
            denom = jnp.sum(weights, axis=1, keepdims=True)
            summed = jnp.dot(weights.astype(jnp.bfloat16), v_head, preferred_element_type=jnp.float32)
            return (summed / denom).astype(jnp.bfloat16)

        heads_out = lax.map(attend, (query_heads, key_heads, value_heads))
        attended = heads_out.transpose(1, 0, 2).reshape(frame_tok, HEADS * HD)
        results.append(jnp.dot(attended, w_out, preferred_element_type=jnp.float32).astype(jnp.bfloat16))
    return jnp.concatenate(results, axis=0)
```

```python
import functools

import jax
import jax.numpy as jnp
from jax import lax
from jax.experimental import pallas as pl
from jax.experimental.pallas import tpu as pltpu
from jax.sharding import PartitionSpec as P

HD = 128
HEADS = 32
FRAMES = 16
BLOCK = 128
KEY_SPLIT = 4
NEG = -1e30
FLOOR = -1e29
MESH = pl.DeviceIdType.MESH


def nt(a, b):
    return lax.dot_general(a, b, (((1,), (1,)), ((), ())), preferred_element_type=jnp.float32)


def tn(a, b):
    return lax.dot_general(a, b, (((0,), (0,)), ((), ())), preferred_element_type=jnp.float32)


def kernel(
    n_t, n_a, n_b,
    tok_ref, wq_ref, wo_ref, k_ref, v_ref, bias_ref,
    fin,
    tz, tg, wq, kg, vg, wo, qp, qr, qs, qa, s_buf, o_s, o_g, st_s, st_g, az_s, az, ag, cs,
    tz_s, tz_r, tg_s, tg_r, wq_s, wq_r, kg_s, kg_r, vg_s, vg_r, wo_r,
    qr_s, qr_r, qa_s, qa_r, os_s, os_r, ss_s, ss_r, az_ss, az_r, ag_s, ag_r, f_s, f_r,
):
    t = lax.axis_index("tm")
    s = lax.axis_index("seq")
    a = s // n_b
    b = lax.rem(s, n_b)
    n_p = n_t * n_b
    n_s = n_a * n_b
    h = t * n_b + b
    heads = qp.shape[0]
    width = heads * HD
    rows = tok_ref.shape[0]
    depth = tok_ref.shape[1] // n_a
    chunk = qp.shape[2]
    queries = n_a * chunk
    per_group = n_a // n_t
    sends = []

    def plane(d):
        g = lax.rem(h + d, n_p)
        return g, g // n_b, lax.rem(g, n_b)

    def cols(i, size):
        return pl.ds(pl.multiple_of(i * size, size), size)

    def send(src, dst, ss, rs, device):
        c = pltpu.make_async_remote_copy(
            src_ref=src, dst_ref=dst, send_sem=ss, recv_sem=rs,
            device_id=device, device_id_type=MESH,
        )
        c.start()
        sends.append(c)

    def landed(ref, sem):
        pltpu.make_async_copy(ref, ref, sem).wait()

    barrier = pltpu.get_barrier_semaphore()
    for d in range(1, n_p):
        g, t2, b2 = plane(d)
        pl.semaphore_signal(barrier, inc=1, device_id=(t2, a * n_b + b2), device_id_type=MESH)
    for da in range(1, n_a):
        for b2 in range(n_b):
            a2 = lax.rem(a + da, n_a)
            pl.semaphore_signal(barrier, inc=1, device_id=(t, a2 * n_b + b2), device_id_type=MESH)
    own = [
        pltpu.make_async_copy(tok_ref.at[:, cols(a, depth)], tz.at[a], tz_r.at[a]),
        pltpu.make_async_copy(wq_ref.at[:, cols(h, width)], wq.at[b], wq_r.at[b]),
        pltpu.make_async_copy(k_ref.at[:, cols(h, width)], kg.at[h], kg_r.at[h]),
        pltpu.make_async_copy(v_ref.at[:, cols(h, width)], vg.at[h], vg_r.at[h]),
    ]
    for c in own:
        c.start()
    wo_copy = pltpu.make_async_copy(wo_ref, wo, wo_r)
    wo_copy.start()
    pl.semaphore_wait(barrier, n_p - 1 + (n_a - 1) * n_b)

    for da in range(1, n_a):
        a2 = lax.rem(a + da, n_a)
        send(tok_ref.at[:, cols(a2, depth)], tz.at[a], tz_s.at[da], tz_r.at[a], (t, a2 * n_b + b))
    for db in range(1, n_b):
        b2 = lax.rem(b + db, n_b)
        send(
            wq_ref.at[:, cols(t * n_b + b2, width)], wq.at[b], wq_s.at[db], wq_r.at[b],
            (t, a * n_b + b2),
        )
    for i in range(n_a):
        landed(tz.at[i], tz_r.at[i])
    own_tok = pltpu.make_async_copy(tz, tg.at[t, :, b], tg_r.at[h])
    own_tok.start()
    for d in range(1, n_p):
        g, t2, b2 = plane(d)
        send(tz, tg.at[t, :, b], tg_s.at[d], tg_r.at[h], (t2, a * n_b + b2))
    for src, dst, ss, rs in ((k_ref, kg, kg_s, kg_r), (v_ref, vg, vg_s, vg_r)):
        for d in range(1, n_p):
            g, t2, b2 = plane(d)
            send(src.at[:, cols(g, width)], dst.at[h], ss.at[d], rs.at[h], (t2, a * n_b + b2))
    for i in range(n_b):
        landed(wq.at[i], wq_r.at[i])
    for i in range(n_p):
        landed(tg.at[i // n_b, :, i % n_b], tg_r.at[i])

    for j in range(heads):
        w_j = wq[:, :, j * HD:(j + 1) * HD].reshape(depth, HD)
        for c in range(n_a):
            piece = tg.at[c // per_group][
                (c % per_group) * (n_a // per_group):(c % per_group + 1) * (n_a // per_group)
            ]
            qp[j, c] = jnp.dot(
                piece.reshape(chunk, depth), w_j, preferred_element_type=jnp.float32
            )
        for da in range(1, n_a):
            a2 = lax.rem(a + da, n_a)
            send(
                qp.at[j, a2], qr.at[j, a], qr_s.at[j, da], qr_r.at[j, a], (t, a2 * n_b + b)
            )
        qr[j, a] = qp[j, a]
    for j in range(heads):
        for da in range(1, n_a):
            a2 = lax.rem(a + da, n_a)
            landed(qr.at[j, a2], qr_r.at[j, a2])
        total = qr[j, 0]
        for i in range(1, n_a):
            total = total + qr[j, i]
        total = total.astype(jnp.bfloat16)
        qs[j] = total
        for da in range(1, n_a):
            a2 = lax.rem(a + da, n_a)
            send(qs.at[j], qa.at[j, a], qa_s.at[j, da], qa_r.at[j, a], (t, a2 * n_b + b))
        qa[j, a] = total

    for i in range(n_p):
        landed(kg.at[i], kg_r.at[i])

    def attend(j):
        lanes = slice(j * HD, (j + 1) * HD)
        for da in range(1, n_a):
            a2 = lax.rem(a + da, n_a)
            landed(qa.at[j, a2], qa_r.at[j, a2])
        q_j = qa[j].reshape(queries, HD)

        def score(i, high):
            sc = nt(kg[i, :, lanes], q_j) * (HD ** -0.5) + bias_ref[pl.ds(i, 1), :]
            s_buf[i] = sc
            return jnp.maximum(high, jnp.max(sc, axis=0, keepdims=True))

        high = lax.fori_loop(0, n_p, score, jnp.full((1, queries), FLOOR, jnp.float32))
        if j == 0:
            for i in range(n_p):
                landed(vg.at[i], vg_r.at[i])

        def mix(i, state):
            denom, acc = state
            w = jnp.exp(s_buf[i] - high)
            return (
                denom + jnp.sum(w, axis=0, keepdims=True),
                acc + tn(vg[i, :, lanes], w.astype(jnp.bfloat16)),
            )

        denom, acc = lax.fori_loop(
            0, n_p, mix,
            (jnp.zeros((1, queries), jnp.float32), jnp.zeros((HD, queries), jnp.float32)),
        )
        out = (acc / jnp.where(denom > 0.0, denom, 1.0)).astype(jnp.bfloat16)
        for c in range(n_a):
            lo = c * chunk
            o_s[j, c] = out[:, lo:lo + chunk]
            st_s[j, c, 0:1] = high[:, lo:lo + chunk]
            st_s[j, c, 1:2] = denom[:, lo:lo + chunk]
            st_s[j, c, 2:8] = jnp.zeros((6, chunk), jnp.float32)
        for da in range(1, n_a):
            a2 = lax.rem(a + da, n_a)
            there = (t, a2 * n_b + b)
            send(o_s.at[j, a2], o_g.at[j, a], os_s.at[j, da], os_r.at[j, a], there)
            send(st_s.at[j, a2], st_g.at[j, a], ss_s.at[j, da], ss_r.at[j, a], there)
        o_g[j, a] = o_s[j, a]
        st_g[j, a] = st_s[j, a]

    def combine(j):
        for da in range(1, n_a):
            a2 = lax.rem(a + da, n_a)
            landed(o_g.at[j, a2], os_r.at[j, a2])
            landed(st_g.at[j, a2], ss_r.at[j, a2])
        high = st_g[j, 0, 0:1]
        for i in range(1, n_a):
            high = jnp.maximum(high, st_g[j, i, 0:1])
        den = jnp.zeros((1, chunk), jnp.float32)
        num = jnp.zeros((HD, chunk), jnp.float32)
        for i in range(n_a):
            w = st_g[j, i, 1:2] * jnp.exp(st_g[j, i, 0:1] - high)
            den = den + w
            num = num + w * o_g[j, i].astype(jnp.float32)
        res = jnp.transpose(num / den).astype(jnp.bfloat16)
        az_s[j] = res
        for da in range(1, n_a):
            a2 = lax.rem(a + da, n_a)
            send(az_s.at[j], az.at[j, a], az_ss.at[j, da], az_r.at[j, a], (t, a2 * n_b + b))
        az[j, a] = res

    def spread(j):
        for da in range(1, n_a):
            a2 = lax.rem(a + da, n_a)
            landed(az.at[j, a2], az_r.at[j, a2])
        for d in range(1, n_p):
            g, t2, b2 = plane(d)
            send(
                az.at[j, pl.ds(t2 * per_group, per_group)], ag.at[j, h],
                ag_s.at[j, d], ag_r.at[j, h], (t2, a * n_b + b2),
            )
        ag[j, h] = az[j, pl.ds(t * per_group, per_group)]

    for j in range(heads):
        attend(j)
        if j >= 1:
            combine(j - 1)
        if j >= 2:
            spread(j - 2)
    combine(heads - 1)
    if heads >= 2:
        spread(heads - 2)
    spread(heads - 1)

    wo_copy.wait()
    group_rows = per_group * chunk
    total = jnp.zeros((group_rows, wo.shape[1]), jnp.float32)
    for j in range(heads):
        for d in range(1, n_p):
            g, t2, b2 = plane(d)
            landed(ag.at[j, g], ag_r.at[j, g])

        def part(i, acc, j=j):
            at = pl.multiple_of(i * width + j * HD, HD)
            return acc + jnp.dot(
                ag[j, i].reshape(group_rows, HD), wo[pl.ds(at, HD), :],
                preferred_element_type=jnp.float32,
            )

        total = lax.fori_loop(0, n_p, part, total)
    cs[...] = total.astype(jnp.bfloat16).reshape(cs.shape)
    for d in range(1, n_s):
        s2 = lax.rem(s + d, n_s)
        send(cs.at[s2], fin.at[s], f_s.at[d], f_r.at[s], (t, s2))
    fin[s] = cs[s]
    for d in range(1, n_s):
        s2 = lax.rem(s + d, n_s)
        landed(fin.at[s2], f_r.at[s2])
    for c in sends:
        c.wait_send()


def on_device(tokens, w_query, w_out, k_cache, v_cache, radial_mask, slot_frame):
    n_s = lax.axis_size("seq")
    n_t = lax.axis_size("tm")
    n_a = KEY_SPLIT
    n_b = n_s // n_a
    n_p = n_t * n_b
    heads = HEADS // n_p
    width = heads * HD
    rows, d_model = tokens.shape
    depth = d_model // n_a
    queries = n_t * n_s * rows
    chunk = queries // n_a
    per_group = n_a // n_t
    keys = k_cache.shape[0]
    w_rows = w_query.shape[0]
    out_cols = w_out.shape[1]
    fb = radial_mask.shape[1]
    slots = slot_frame.shape[0]
    a = lax.axis_index("seq") // n_b

    onehot = (slot_frame[:, None] == lax.iota(jnp.int32, slots)[None, :]).astype(jnp.float32)
    frames = onehot.reshape(n_t, slots // n_t, slots)[:, 0]
    chosen = jnp.einsum("gf,fqk->gqk", frames, radial_mask.astype(jnp.float32))
    chosen = chosen.reshape(n_t * fb, slots, fb)
    by_slot = jnp.einsum("sf,qfb->sbq", onehot, chosen)
    tiles = by_slot.reshape(n_t, n_a, n_b, n_t * fb)
    mine = lax.dynamic_index_in_dim(tiles, a, 1, keepdims=False).reshape(n_p, n_t * fb)
    bias = jnp.repeat(jnp.where(mine > 0.5, 0.0, NEG), BLOCK, axis=1)

    bf, f32 = jnp.bfloat16, jnp.float32
    vm, dma = pltpu.VMEM, pltpu.SemaphoreType.DMA
    hbm = pl.BlockSpec(memory_space=pl.ANY)
    vmem = pl.BlockSpec(memory_space=pltpu.VMEM)
    got = pl.pallas_call(
        functools.partial(kernel, n_t, n_a, n_b),
        out_shape=jax.ShapeDtypeStruct((n_s, rows, out_cols), bf),
        in_specs=[hbm] * 5 + [vmem],
        out_specs=vmem,
        scratch_shapes=[
            vm((n_a, rows, depth), bf),
            vm((n_t, n_a, n_b, rows, depth), bf),
            vm((n_b, w_rows, width), bf),
            vm((n_p, keys, width), bf),
            vm((n_p, keys, width), bf),
            vm(w_out.shape, bf),
            vm((heads, n_a, chunk, HD), f32),
            vm((heads, n_a, chunk, HD), f32),
            vm((heads, chunk, HD), bf),
            vm((heads, n_a, chunk, HD), bf),
            vm((n_p, keys, queries), f32),
            vm((heads, n_a, HD, chunk), bf),
            vm((heads, n_a, HD, chunk), bf),
            vm((heads, n_a, 8, chunk), f32),
            vm((heads, n_a, 8, chunk), f32),
            vm((heads, chunk, HD), bf),
            vm((heads, n_a, chunk, HD), bf),
            vm((heads, n_p, per_group, chunk, HD), bf),
            vm((n_s, rows, out_cols), bf),
            dma((n_a,)), dma((n_a,)),
            dma((n_p,)), dma((n_p,)),
            dma((n_b,)), dma((n_b,)),
            dma((n_p,)), dma((n_p,)),
            dma((n_p,)), dma((n_p,)),
            dma,
            dma((heads, n_a)), dma((heads, n_a)),
            dma((heads, n_a)), dma((heads, n_a)),
            dma((heads, n_a)), dma((heads, n_a)),
            dma((heads, n_a)), dma((heads, n_a)),
            dma((heads, n_a)), dma((heads, n_a)),
            dma((heads, n_p)), dma((heads, n_p)),
            dma((n_s,)), dma((n_s,)),
        ],
        compiler_params=pltpu.CompilerParams(
            collective_id=0, has_side_effects=True, vmem_limit_bytes=60 * 1024 * 1024
        ),
    )(tokens, w_query, w_out, k_cache, v_cache, bias)
    return got.transpose(1, 0, 2).reshape(rows, n_s * out_cols)


def solution(mesh):
    return jax.shard_map(
        on_device,
        mesh=mesh,
        in_specs=(
            P(("tm", "seq"), None),
            P("seq", None),
            P(None, "seq"),
            P(("tm", "seq"), None),
            P(("tm", "seq"), None),
            P(),
            P(),
        ),
        out_specs=P(("tm", "seq"), None),
        check_vma=False,
    )
```

```python
import functools

import jax
import jax.numpy as jnp
from jax import lax
from jax.experimental import pallas as pl
from jax.experimental.pallas import tpu as pltpu
from jax.sharding import PartitionSpec as P

HD = 128
HEADS = 32
FRAMES = 16
BLOCK = 128
KEY_SPLIT = 4
NEG = -1e30
FLOOR = -1e29
CORES = 2
MESH = pl.DeviceIdType.MESH


def nt(a, b):
    return lax.dot_general(a, b, (((1,), (1,)), ((), ())), preferred_element_type=jnp.float32)


def tn(a, b):
    return lax.dot_general(a, b, (((0,), (0,)), ((), ())), preferred_element_type=jnp.float32)


def kernel(
    n_t, n_a, n_b,
    tok_ref, wq_ref, wo_ref, k_ref, v_ref, mask_ref, frame_ref,
    out_ref,
    bias_ref, fin, tz, tg, wq, kg, vg, wo, qp, qr, qs, qa, s_buf, o_s, o_g, st_s, st_g, az_s, az, ag, cs,
    tz_s, tz_r, tg_s, tg_r, tf_s, wq_s, wq_r, kg_s, kg_r, vg_s, vg_r, wo_r,
    qr_s, qr_r, qa_s, qa_r, os_s, os_r, ss_s, ss_r, az_ss, az_r, ag_s, ag_r, af_s, f_s, f_r,
):
    t = lax.axis_index("tm")
    s = lax.axis_index("seq")
    a = s // n_b
    b = lax.rem(s, n_b)
    n_p = n_t * n_b
    n_s = n_a * n_b
    h = t * n_b + b
    heads = qp.shape[0]
    width = heads * HD
    rows = tok_ref.shape[0]
    depth = tok_ref.shape[1] // n_a
    chunk = qp.shape[2]
    queries = n_a * chunk
    per_group = n_a // n_t
    sends = []

    def plane(d):
        g = lax.rem(h + d, n_p)
        return g, g // n_b, lax.rem(g, n_b)

    core = lax.rem(b, CORES)
    mate = b - core + (CORES - 1 - core)
    n_c = n_p // CORES
    chip = h // CORES

    def same_core(d):
        g = lax.rem(chip + d, n_c) * CORES + core
        return g, g // n_b, lax.rem(g, n_b)

    def cols(i, size):
        return pl.ds(pl.multiple_of(i * size, size), size)

    def send(src, dst, ss, rs, device):
        c = pltpu.make_async_remote_copy(
            src_ref=src, dst_ref=dst, send_sem=ss, recv_sem=rs,
            device_id=device, device_id_type=MESH,
        )
        c.start()
        sends.append(c)

    def landed(ref, sem):
        pltpu.make_async_copy(ref, ref, sem).wait()

    barrier = pltpu.get_barrier_semaphore()
    for d in range(1, n_p):
        g, t2, b2 = plane(d)
        pl.semaphore_signal(barrier, inc=1, device_id=(t2, a * n_b + b2), device_id_type=MESH)
    for da in range(1, n_a):
        for b2 in range(n_b):
            a2 = lax.rem(a + da, n_a)
            pl.semaphore_signal(barrier, inc=1, device_id=(t, a2 * n_b + b2), device_id_type=MESH)
    own = [
        pltpu.make_async_copy(tok_ref.at[:, cols(a, depth)], tz.at[a], tz_r.at[a]),
        pltpu.make_async_copy(wq_ref.at[:, cols(h, width)], wq.at[b], wq_r.at[b]),
        pltpu.make_async_copy(k_ref.at[:, cols(h, width)], kg.at[h], kg_r.at[h]),
        pltpu.make_async_copy(v_ref.at[:, cols(h, width)], vg.at[h], vg_r.at[h]),
    ]
    for c in own:
        c.start()
    wo_copy = pltpu.make_async_copy(wo_ref, wo, wo_r)
    wo_copy.start()
    pl.semaphore_wait(barrier, n_p - 1 + (n_a - 1) * n_b)

    for da in range(1, n_a):
        a2 = lax.rem(a + da, n_a)
        send(tok_ref.at[:, cols(a2, depth)], tz.at[a], tz_s.at[da], tz_r.at[a], (t, a2 * n_b + b))
    for db in range(1, n_b):
        b2 = lax.rem(b + db, n_b)
        send(
            wq_ref.at[:, cols(t * n_b + b2, width)], wq.at[b], wq_s.at[db], wq_r.at[b],
            (t, a * n_b + b2),
        )
    for i in range(n_a):
        landed(tz.at[i], tz_r.at[i])
    own_tok = pltpu.make_async_copy(tz, tg.at[t, :, b], tg_r.at[h])
    own_tok.start()
    for d in range(1, n_c):
        g, t2, b2 = same_core(d)
        send(tz, tg.at[t, :, b], tg_s.at[d], tg_r.at[h], (t2, a * n_b + b2))
    send(tz, tg.at[t, :, b], tg_s.at[0], tg_r.at[h], (t, a * n_b + mate))
    for src, dst, ss, rs in ((k_ref, kg, kg_s, kg_r), (v_ref, vg, vg_s, vg_r)):
        for d in range(1, n_p):
            g, t2, b2 = plane(d)
            send(src.at[:, cols(g, width)], dst.at[h], ss.at[d], rs.at[h], (t2, a * n_b + b2))
    slots = frame_ref.shape[0]
    tiles = mask_ref.shape[1]

    def allow(i, carry):
        tile = (i // n_b) * n_s + a * n_b + lax.rem(i, n_b)
        column = frame_ref[tile // tiles] * tiles + lax.rem(tile, tiles)
        for g in range(n_t):
            frame = frame_ref[g * (slots // n_t)]
            for r in range(tiles):
                lo = (g * tiles + r) * BLOCK
                value = jnp.where(mask_ref[frame, r, column] > 0, 0.0, NEG)
                bias_ref[i, :, lo:lo + BLOCK] = jnp.full((1, BLOCK), value, jnp.float32)
        return carry

    lax.fori_loop(0, n_p, allow, 0)
    for d in range(1, n_c):
        g, t2, b2 = same_core(d)
        landed(tg.at[t2, :, b2], tg_r.at[g])
        send(tg.at[t2, :, b2], tg.at[t2, :, b2], tf_s.at[d], tg_r.at[g], (t, a * n_b + mate))
    for i in range(n_b):
        landed(wq.at[i], wq_r.at[i])
    landed(tg.at[t, :, b], tg_r.at[h])
    for d in range(n_c):
        g, t2, b2 = same_core(d)
        b3 = b2 - core + (CORES - 1 - core)
        landed(tg.at[t2, :, b3], tg_r.at[t2 * n_b + b3])

    for j in range(heads):
        w_j = wq[:, :, j * HD:(j + 1) * HD].reshape(depth, HD)
        for c in range(n_a):
            piece = tg.at[c // per_group][
                (c % per_group) * (n_a // per_group):(c % per_group + 1) * (n_a // per_group)
            ]
            qp[j, c] = jnp.dot(
                piece.reshape(chunk, depth), w_j, preferred_element_type=jnp.float32
            )
        for da in range(1, n_a):
            a2 = lax.rem(a + da, n_a)
            send(
                qp.at[j, a2], qr.at[j, a], qr_s.at[j, da], qr_r.at[j, a], (t, a2 * n_b + b)
            )
        qr[j, a] = qp[j, a]
    for j in range(heads):
        for da in range(1, n_a):
            a2 = lax.rem(a + da, n_a)
            landed(qr.at[j, a2], qr_r.at[j, a2])
        total = qr[j, 0]
        for i in range(1, n_a):
            total = total + qr[j, i]
        total = total.astype(jnp.bfloat16)
        qs[j] = total
        for da in range(1, n_a):
            a2 = lax.rem(a + da, n_a)
            send(qs.at[j], qa.at[j, a], qa_s.at[j, da], qa_r.at[j, a], (t, a2 * n_b + b))
        qa[j, a] = total

    for i in range(n_p):
        landed(kg.at[i], kg_r.at[i])

    def attend(j):
        lanes = slice(j * HD, (j + 1) * HD)
        for da in range(1, n_a):
            a2 = lax.rem(a + da, n_a)
            landed(qa.at[j, a2], qa_r.at[j, a2])
        q_j = qa[j].reshape(queries, HD)

        def score(i, high):
            sc = nt(kg[i, :, lanes], q_j) * (HD ** -0.5) + bias_ref[i]
            s_buf[i] = sc
            return jnp.maximum(high, jnp.max(sc, axis=0, keepdims=True))

        high = lax.fori_loop(0, n_p, score, jnp.full((1, queries), FLOOR, jnp.float32))
        if j == 0:
            for i in range(n_p):
                landed(vg.at[i], vg_r.at[i])

        def mix(i, state):
            denom, acc = state
            w = jnp.exp(s_buf[i] - high)
            return (
                denom + jnp.sum(w, axis=0, keepdims=True),
                acc + tn(vg[i, :, lanes], w.astype(jnp.bfloat16)),
            )

        denom, acc = lax.fori_loop(
            0, n_p, mix,
            (jnp.zeros((1, queries), jnp.float32), jnp.zeros((HD, queries), jnp.float32)),
        )
        out = (acc / jnp.where(denom > 0.0, denom, 1.0)).astype(jnp.bfloat16)
        for c in range(n_a):
            lo = c * chunk
            o_s[j, c] = out[:, lo:lo + chunk]
            st_s[j, c, 0:1] = high[:, lo:lo + chunk]
            st_s[j, c, 1:2] = denom[:, lo:lo + chunk]
            st_s[j, c, 2:8] = jnp.zeros((6, chunk), jnp.float32)
        for da in range(1, n_a):
            a2 = lax.rem(a + da, n_a)
            there = (t, a2 * n_b + b)
            send(o_s.at[j, a2], o_g.at[j, a], os_s.at[j, da], os_r.at[j, a], there)
            send(st_s.at[j, a2], st_g.at[j, a], ss_s.at[j, da], ss_r.at[j, a], there)
        o_g[j, a] = o_s[j, a]
        st_g[j, a] = st_s[j, a]

    def combine(j):
        for da in range(1, n_a):
            a2 = lax.rem(a + da, n_a)
            landed(o_g.at[j, a2], os_r.at[j, a2])
            landed(st_g.at[j, a2], ss_r.at[j, a2])
        high = st_g[j, 0, 0:1]
        for i in range(1, n_a):
            high = jnp.maximum(high, st_g[j, i, 0:1])
        den = jnp.zeros((1, chunk), jnp.float32)
        num = jnp.zeros((HD, chunk), jnp.float32)
        for i in range(n_a):
            w = st_g[j, i, 1:2] * jnp.exp(st_g[j, i, 0:1] - high)
            den = den + w
            num = num + w * o_g[j, i].astype(jnp.float32)
        res = jnp.transpose(num / den).astype(jnp.bfloat16)
        az_s[j] = res
        for da in range(1, n_a):
            a2 = lax.rem(a + da, n_a)
            send(az_s.at[j], az.at[j, a], az_ss.at[j, da], az_r.at[j, a], (t, a2 * n_b + b))
        az[j, a] = res

    def spread(j):
        for da in range(1, n_a):
            a2 = lax.rem(a + da, n_a)
            landed(az.at[j, a2], az_r.at[j, a2])
        for d in range(n_c):
            g, t2, b2 = same_core(d)
            send(
                az.at[j, pl.ds(t2 * per_group, per_group)], ag.at[j, h],
                ag_s.at[j, d], ag_r.at[j, h], (t2, a * n_b + (b2 if d else mate)),
            )
        ag[j, h] = az[j, pl.ds(t * per_group, per_group)]

    def forward(j):
        for d in range(1, n_c):
            g, t2, b2 = same_core(d)
            landed(ag.at[j, g], ag_r.at[j, g])
            send(ag.at[j, g], ag.at[j, g], af_s.at[j, d], ag_r.at[j, g], (t, a * n_b + mate))

    for j in range(heads):
        attend(j)
        if j >= 1:
            combine(j - 1)
        if j >= 2:
            spread(j - 2)
        if j >= 3:
            forward(j - 3)
    combine(heads - 1)
    if heads >= 2:
        spread(heads - 2)
    spread(heads - 1)
    for j in range(max(0, heads - 3), heads):
        forward(j)

    wo_copy.wait()
    group_rows = per_group * chunk
    total = jnp.zeros((group_rows, wo.shape[0]), jnp.float32)
    for j in range(heads):
        for d in range(n_c):
            g, t2, b2 = same_core(d)
            g3 = g - core + (CORES - 1 - core)
            landed(ag.at[j, g3], ag_r.at[j, g3])

        def part(i, acc, j=j):
            at = pl.multiple_of(i * width + j * HD, HD)
            return acc + nt(ag[j, i].reshape(group_rows, HD), wo[:, pl.ds(at, HD)])

        total = lax.fori_loop(0, n_p, part, total)
    cs[...] = total.astype(jnp.bfloat16).reshape(cs.shape)
    for d in range(1, n_s):
        s2 = lax.rem(s + d, n_s)
        send(cs.at[s2], fin.at[s], f_s.at[d], f_r.at[s], (t, s2))
    fin[s] = cs[s]
    for d in range(1, n_s):
        s2 = lax.rem(s + d, n_s)
        landed(fin.at[s2], f_r.at[s2])
    wide = fin.shape[2]
    for i in range(n_s):
        out_ref[:, i * wide:(i + 1) * wide] = fin[i]
    for c in sends:
        c.wait_send()


def on_device(tokens, w_query, w_out, k_cache, v_cache, radial_mask, slot_frame):
    n_s = lax.axis_size("seq")
    n_t = lax.axis_size("tm")
    n_a = KEY_SPLIT
    n_b = n_s // n_a
    n_p = n_t * n_b
    heads = HEADS // n_p
    width = heads * HD
    rows, d_model = tokens.shape
    depth = d_model // n_a
    queries = n_t * n_s * rows
    chunk = queries // n_a
    per_group = n_a // n_t
    keys = k_cache.shape[0]
    w_rows = w_query.shape[0]
    out_cols = w_out.shape[1]

    bf, f32 = jnp.bfloat16, jnp.float32
    vm, dma = pltpu.VMEM, pltpu.SemaphoreType.DMA
    hbm = pl.BlockSpec(memory_space=pl.ANY)
    vmem = pl.BlockSpec(memory_space=pltpu.VMEM)
    smem = pl.BlockSpec(memory_space=pltpu.SMEM)
    return pl.pallas_call(
        functools.partial(kernel, n_t, n_a, n_b),
        out_shape=jax.ShapeDtypeStruct((rows, n_s * out_cols), bf),
        in_specs=[hbm] * 5 + [smem] * 2,
        out_specs=vmem,
        scratch_shapes=[
            vm((n_p, 1, queries), f32),
            vm((n_s, rows, out_cols), bf),
            vm((n_a, rows, depth), bf),
            vm((n_t, n_a, n_b, rows, depth), bf),
            vm((n_b, w_rows, width), bf),
            vm((n_p, keys, width), bf),
            vm((n_p, keys, width), bf),
            vm(w_out.shape[::-1], bf),
            vm((heads, n_a, chunk, HD), f32),
            vm((heads, n_a, chunk, HD), f32),
            vm((heads, chunk, HD), bf),
            vm((heads, n_a, chunk, HD), bf),
            vm((n_p, keys, queries), f32),
            vm((heads, n_a, HD, chunk), bf),
            vm((heads, n_a, HD, chunk), bf),
            vm((heads, n_a, 8, chunk), f32),
            vm((heads, n_a, 8, chunk), f32),
            vm((heads, chunk, HD), bf),
            vm((heads, n_a, chunk, HD), bf),
            vm((heads, n_p, per_group, chunk, HD), bf),
            vm((n_s, rows, out_cols), bf),
            dma((n_a,)), dma((n_a,)),
            dma((n_p,)), dma((n_p,)), dma((n_p,)),
            dma((n_b,)), dma((n_b,)),
            dma((n_p,)), dma((n_p,)),
            dma((n_p,)), dma((n_p,)),
            dma,
            dma((heads, n_a)), dma((heads, n_a)),
            dma((heads, n_a)), dma((heads, n_a)),
            dma((heads, n_a)), dma((heads, n_a)),
            dma((heads, n_a)), dma((heads, n_a)),
            dma((heads, n_a)), dma((heads, n_a)),
            dma((heads, n_p)), dma((heads, n_p)), dma((heads, n_p)),
            dma((n_s,)), dma((n_s,)),
        ],
        compiler_params=pltpu.CompilerParams(
            collective_id=0, has_side_effects=True, vmem_limit_bytes=60 * 1024 * 1024
        ),
    )(tokens, w_query, w_out.T, k_cache, v_cache, radial_mask, slot_frame)


def solution(mesh):
    return jax.shard_map(
        on_device,
        mesh=mesh,
        in_specs=(
            P(("tm", "seq"), None),
            P("seq", None),
            P(None, "seq"),
            P(("tm", "seq"), None),
            P(("tm", "seq"), None),
            P(),
            P(),
        ),
        out_specs=P(("tm", "seq"), None),
        check_vma=False,
    )
```

```python
import functools

import jax
import jax.numpy as jnp
from jax import lax
from jax.experimental import pallas as pl
from jax.experimental.pallas import tpu as pltpu
from jax.sharding import PartitionSpec as P

HD = 128
HEADS = 32
FRAMES = 16
BLOCK = 128
KEY_SPLIT = 4
NEG = -1e30
FLOOR = -1e29
CORES = 2
MESH = pl.DeviceIdType.MESH


def nt(a, b):
    return lax.dot_general(a, b, (((1,), (1,)), ((), ())), preferred_element_type=jnp.float32)


def tn(a, b):
    return lax.dot_general(a, b, (((0,), (0,)), ((), ())), preferred_element_type=jnp.float32)


def kernel(
    n_t, n_a, n_b,
    tok_ref, wq_ref, wo_ref, k_ref, v_ref, mask_ref, frame_ref,
    out_ref,
    bias_ref, fin, tz, tg, wq, kg, vg, wo, qp, r1, x1, r2, qs, qa, s_buf, o_s, o_g, st_s, st_g, az_s, az, ag, cs,
    tz_s, tz_r, tg_s, tg_r, tf_s, wq_s, wq_r, kg_s, kg_r, vg_s, vg_r, wo_r,
    r1_s, r1_r, r2_s, r2_r, qa_s, qa_r, os_s, os_r, ss_s, ss_r, az_ss, az_r, ag_s, ag_r, af_s, f_s, f_r,
):
    t = lax.axis_index("tm")
    s = lax.axis_index("seq")
    a = s // n_b
    b = lax.rem(s, n_b)
    n_p = n_t * n_b
    n_s = n_a * n_b
    h = t * n_b + b
    heads = qp.shape[0]
    width = heads * HD
    rows = tok_ref.shape[0]
    depth = tok_ref.shape[1] // n_a
    chunk = qp.shape[3]
    queries = n_a * chunk
    per_group = n_a // n_t
    low = lax.rem(a, 2)
    high_half = a // 2
    beside = (t, (2 * high_half + 1 - low) * n_b + b)
    across = (t, (2 * (1 - high_half) + low) * n_b + b)
    sends = []

    def plane(d):
        g = lax.rem(h + d, n_p)
        return g, g // n_b, lax.rem(g, n_b)

    core = lax.rem(b, CORES)
    mate = b - core + (CORES - 1 - core)
    n_c = n_p // CORES
    chip = h // CORES

    def same_core(d):
        g = lax.rem(chip + d, n_c) * CORES + core
        return g, g // n_b, lax.rem(g, n_b)

    def slab(j, g):
        return ag.at[:, :, pl.ds(pl.multiple_of(g * width + j * HD, HD), HD)]

    def cols(i, size):
        return pl.ds(pl.multiple_of(i * size, size), size)

    def send(src, dst, ss, rs, device):
        c = pltpu.make_async_remote_copy(
            src_ref=src, dst_ref=dst, send_sem=ss, recv_sem=rs,
            device_id=device, device_id_type=MESH,
        )
        c.start()
        sends.append(c)

    def landed(ref, sem):
        pltpu.make_async_copy(ref, ref, sem).wait()

    barrier = pltpu.get_barrier_semaphore()
    for d in range(1, n_p):
        g, t2, b2 = plane(d)
        pl.semaphore_signal(barrier, inc=1, device_id=(t2, a * n_b + b2), device_id_type=MESH)
    for da in range(1, n_a):
        for b2 in range(n_b):
            a2 = lax.rem(a + da, n_a)
            pl.semaphore_signal(barrier, inc=1, device_id=(t, a2 * n_b + b2), device_id_type=MESH)
    own = [
        pltpu.make_async_copy(tok_ref.at[:, cols(a, depth)], tz.at[a], tz_r.at[a]),
        pltpu.make_async_copy(wq_ref.at[:, cols(h, width)], wq.at[b], wq_r.at[b]),
        pltpu.make_async_copy(k_ref.at[:, cols(h, width)], kg.at[h], kg_r.at[h]),
        pltpu.make_async_copy(v_ref.at[:, cols(h, width)], vg.at[h], vg_r.at[h]),
    ]
    for c in own:
        c.start()
    wo_copy = pltpu.make_async_copy(wo_ref, wo, wo_r)
    wo_copy.start()
    pl.semaphore_wait(barrier, n_p - 1 + (n_a - 1) * n_b)

    for da in range(1, n_a):
        a2 = lax.rem(a + da, n_a)
        send(tok_ref.at[:, cols(a2, depth)], tz.at[a], tz_s.at[da], tz_r.at[a], (t, a2 * n_b + b))
    for db in range(1, n_b):
        b2 = lax.rem(b + db, n_b)
        send(
            wq_ref.at[:, cols(t * n_b + b2, width)], wq.at[b], wq_s.at[db], wq_r.at[b],
            (t, a * n_b + b2),
        )
    for i in range(n_a):
        landed(tz.at[i], tz_r.at[i])
    own_tok = pltpu.make_async_copy(tz, tg.at[t, :, b], tg_r.at[h])
    own_tok.start()
    for d in range(1, n_c):
        g, t2, b2 = same_core(d)
        send(tz, tg.at[t, :, b], tg_s.at[d], tg_r.at[h], (t2, a * n_b + b2))
    send(tz, tg.at[t, :, b], tg_s.at[0], tg_r.at[h], (t, a * n_b + mate))
    slots = frame_ref.shape[0]
    tiles = mask_ref.shape[1]

    def allow(i, carry):
        tile = (i // n_b) * n_s + a * n_b + lax.rem(i, n_b)
        column = frame_ref[tile // tiles] * tiles + lax.rem(tile, tiles)
        for g in range(n_t):
            frame = frame_ref[g * (slots // n_t)]
            for r in range(tiles):
                lo = (g * tiles + r) * BLOCK
                value = jnp.where(mask_ref[frame, r, column] > 0, 0.0, NEG)
                bias_ref[i, :, lo:lo + BLOCK] = jnp.full((1, BLOCK), value, jnp.float32)
        return carry

    lax.fori_loop(0, n_p, allow, 0)
    for d in range(1, n_c):
        g, t2, b2 = same_core(d)
        landed(tg.at[t2, :, b2], tg_r.at[g])
        send(tg.at[t2, :, b2], tg.at[t2, :, b2], tf_s.at[d], tg_r.at[g], (t, a * n_b + mate))
    for i in range(n_b):
        landed(wq.at[i], wq_r.at[i])
    landed(tg.at[t, :, b], tg_r.at[h])
    for d in range(n_c):
        g, t2, b2 = same_core(d)
        b3 = b2 - core + (CORES - 1 - core)
        landed(tg.at[t2, :, b3], tg_r.at[t2 * n_b + b3])

    for src, dst, ss, rs in ((k_ref, kg, kg_s, kg_r), (v_ref, vg, vg_s, vg_r)):
        for d in range(1, n_p):
            g, t2, b2 = plane(d)
            send(src.at[:, cols(g, width)], dst.at[h], ss.at[d], rs.at[h], (t2, a * n_b + b2))

    for j in range(heads):
        w_j = wq[:, :, j * HD:(j + 1) * HD].reshape(depth, HD)
        for c in range(n_a):
            piece = tg.at[c // per_group][
                (c % per_group) * (n_a // per_group):(c % per_group + 1) * (n_a // per_group)
            ]
            qp[j, c // 2, c % 2] = jnp.dot(
                piece.reshape(chunk, depth), w_j, preferred_element_type=jnp.float32
            )
        send(qp.at[j, :, 1 - low], r1.at[j], r1_s.at[j], r1_r.at[j], beside)
    for j in range(heads):
        landed(r1.at[j], r1_r.at[j])
        x1[j] = qp[j, 1 - high_half, low] + r1[j, 1 - high_half]
        send(x1.at[j], r2.at[j], r2_s.at[j], r2_r.at[j], across)
    for j in range(heads):
        landed(r2.at[j], r2_r.at[j])
        total = qp[j, high_half, low] + r1[j, high_half] + r2[j]
        total = total.astype(jnp.bfloat16)
        qs[j] = total
        for da in range(1, n_a):
            a2 = lax.rem(a + da, n_a)
            send(qs.at[j], qa.at[j, a], qa_s.at[j, da], qa_r.at[j, a], (t, a2 * n_b + b))
        qa[j, a] = total

    for i in range(n_p):
        landed(kg.at[i], kg_r.at[i])

    def attend(j):
        lanes = slice(j * HD, (j + 1) * HD)
        for da in range(1, n_a):
            a2 = lax.rem(a + da, n_a)
            landed(qa.at[j, a2], qa_r.at[j, a2])
        q_j = qa[j].reshape(queries, HD)

        def score(i, high):
            sc = nt(kg[i, :, lanes], q_j) * (HD ** -0.5) + bias_ref[i]
            s_buf[i] = sc
            return jnp.maximum(high, jnp.max(sc, axis=0, keepdims=True))

        high = lax.fori_loop(0, n_p, score, jnp.full((1, queries), FLOOR, jnp.float32))
        if j == 0:
            for i in range(n_p):
                landed(vg.at[i], vg_r.at[i])

        def mix(i, state):
            denom, acc = state
            w = jnp.exp(s_buf[i] - high)
            return (
                denom + jnp.sum(w, axis=0, keepdims=True),
                acc + tn(vg[i, :, lanes], w.astype(jnp.bfloat16)),
            )

        denom, acc = lax.fori_loop(
            0, n_p, mix,
            (jnp.zeros((1, queries), jnp.float32), jnp.zeros((HD, queries), jnp.float32)),
        )
        out = (acc / jnp.where(denom > 0.0, denom, 1.0)).astype(jnp.bfloat16)
        for c in range(n_a):
            lo = c * chunk
            o_s[j, c] = out[:, lo:lo + chunk]
            st_s[j, c, 0:1] = high[:, lo:lo + chunk]
            st_s[j, c, 1:2] = denom[:, lo:lo + chunk]
            st_s[j, c, 2:8] = jnp.zeros((6, chunk), jnp.float32)
        for da in range(1, n_a):
            a2 = lax.rem(a + da, n_a)
            there = (t, a2 * n_b + b)
            send(o_s.at[j, a2], o_g.at[j, a], os_s.at[j, da], os_r.at[j, a], there)
            send(st_s.at[j, a2], st_g.at[j, a], ss_s.at[j, da], ss_r.at[j, a], there)
        o_g[j, a] = o_s[j, a]
        st_g[j, a] = st_s[j, a]

    def combine(j):
        for da in range(1, n_a):
            a2 = lax.rem(a + da, n_a)
            landed(o_g.at[j, a2], os_r.at[j, a2])
            landed(st_g.at[j, a2], ss_r.at[j, a2])
        high = st_g[j, 0, 0:1]
        for i in range(1, n_a):
            high = jnp.maximum(high, st_g[j, i, 0:1])
        den = jnp.zeros((1, chunk), jnp.float32)
        num = jnp.zeros((HD, chunk), jnp.float32)
        for i in range(n_a):
            w = st_g[j, i, 1:2] * jnp.exp(st_g[j, i, 0:1] - high)
            den = den + w
            num = num + w * o_g[j, i].astype(jnp.float32)
        res = jnp.transpose(num / den).astype(jnp.bfloat16)
        az_s[j] = res
        for da in range(1, n_a):
            a2 = lax.rem(a + da, n_a)
            send(az_s.at[j], az.at[j, a], az_ss.at[j, da], az_r.at[j, a], (t, a2 * n_b + b))
        az[j, a] = res

    def spread(j):
        for da in range(1, n_a):
            a2 = lax.rem(a + da, n_a)
            landed(az.at[j, a2], az_r.at[j, a2])
        for d in range(n_c):
            g, t2, b2 = same_core(d)
            send(
                az.at[j, pl.ds(t2 * per_group, per_group)], slab(j, h),
                ag_s.at[j, d], ag_r.at[j, h], (t2, a * n_b + (b2 if d else mate)),
            )
        at = pl.multiple_of(h * width + j * HD, HD)
        ag[:, :, pl.ds(at, HD)] = az[j, pl.ds(t * per_group, per_group)]

    def forward(j):
        for d in range(1, n_c):
            g, t2, b2 = same_core(d)
            landed(slab(j, g), ag_r.at[j, g])
            send(slab(j, g), slab(j, g), af_s.at[j, d], ag_r.at[j, g], (t, a * n_b + mate))

    for j in range(heads):
        attend(j)
        if j >= 1:
            combine(j - 1)
        if j >= 2:
            spread(j - 2)
        if j >= 3:
            forward(j - 3)
    combine(heads - 1)
    if heads >= 2:
        spread(heads - 2)
    spread(heads - 1)
    for j in range(max(0, heads - 3), heads):
        forward(j)

    wo_copy.wait()
    group_rows = per_group * chunk
    for j in range(heads):
        for d in range(n_c):
            g, t2, b2 = same_core(d)
            g3 = g - core + (CORES - 1 - core)
            landed(slab(j, g3), ag_r.at[j, g3])
    total = nt(ag[...].reshape(group_rows, n_p * width), wo[...])
    cs[...] = total.astype(jnp.bfloat16).reshape(cs.shape)
    for d in range(1, n_s):
        s2 = lax.rem(s + d, n_s)
        send(cs.at[s2], fin.at[s], f_s.at[d], f_r.at[s], (t, s2))
    fin[s] = cs[s]
    for d in range(1, n_s):
        s2 = lax.rem(s + d, n_s)
        landed(fin.at[s2], f_r.at[s2])
    wide = fin.shape[2]
    for i in range(n_s):
        out_ref[:, i * wide:(i + 1) * wide] = fin[i]
    for c in sends:
        c.wait_send()


def on_device(tokens, w_query, w_out, k_cache, v_cache, radial_mask, slot_frame):
    n_s = lax.axis_size("seq")
    n_t = lax.axis_size("tm")
    n_a = KEY_SPLIT
    n_b = n_s // n_a
    n_p = n_t * n_b
    heads = HEADS // n_p
    width = heads * HD
    rows, d_model = tokens.shape
    depth = d_model // n_a
    queries = n_t * n_s * rows
    chunk = queries // n_a
    per_group = n_a // n_t
    keys = k_cache.shape[0]
    w_rows = w_query.shape[0]
    out_cols = w_out.shape[1]

    bf, f32 = jnp.bfloat16, jnp.float32
    vm, dma = pltpu.VMEM, pltpu.SemaphoreType.DMA
    hbm = pl.BlockSpec(memory_space=pl.ANY)
    vmem = pl.BlockSpec(memory_space=pltpu.VMEM)
    smem = pl.BlockSpec(memory_space=pltpu.SMEM)
    return pl.pallas_call(
        functools.partial(kernel, n_t, n_a, n_b),
        out_shape=jax.ShapeDtypeStruct((rows, n_s * out_cols), bf),
        in_specs=[hbm] * 5 + [smem] * 2,
        out_specs=vmem,
        scratch_shapes=[
            vm((n_p, 1, queries), f32),
            vm((n_s, rows, out_cols), bf),
            vm((n_a, rows, depth), bf),
            vm((n_t, n_a, n_b, rows, depth), bf),
            vm((n_b, w_rows, width), bf),
            vm((n_p, keys, width), bf),
            vm((n_p, keys, width), bf),
            vm(w_out.shape[::-1], bf),
            vm((heads, 2, 2, chunk, HD), f32),
            vm((heads, 2, chunk, HD), f32),
            vm((heads, chunk, HD), f32),
            vm((heads, chunk, HD), f32),
            vm((heads, chunk, HD), bf),
            vm((heads, n_a, chunk, HD), bf),
            vm((n_p, keys, queries), f32),
            vm((heads, n_a, HD, chunk), bf),
            vm((heads, n_a, HD, chunk), bf),
            vm((heads, n_a, 8, chunk), f32),
            vm((heads, n_a, 8, chunk), f32),
            vm((heads, chunk, HD), bf),
            vm((heads, n_a, chunk, HD), bf),
            vm((per_group, chunk, n_p * width), bf),
            vm((n_s, rows, out_cols), bf),
            dma((n_a,)), dma((n_a,)),
            dma((n_p,)), dma((n_p,)), dma((n_p,)),
            dma((n_b,)), dma((n_b,)),
            dma((n_p,)), dma((n_p,)),
            dma((n_p,)), dma((n_p,)),
            dma,
            dma((heads,)), dma((heads,)), dma((heads,)), dma((heads,)),
            dma((heads, n_a)), dma((heads, n_a)),
            dma((heads, n_a)), dma((heads, n_a)),
            dma((heads, n_a)), dma((heads, n_a)),
            dma((heads, n_a)), dma((heads, n_a)),
            dma((heads, n_p)), dma((heads, n_p)), dma((heads, n_p)),
            dma((n_s,)), dma((n_s,)),
        ],
        compiler_params=pltpu.CompilerParams(
            collective_id=0, has_side_effects=True, vmem_limit_bytes=60 * 1024 * 1024
        ),
    )(tokens, w_query, w_out.T, k_cache, v_cache, radial_mask, slot_frame)


def solution(mesh):
    return jax.shard_map(
        on_device,
        mesh=mesh,
        in_specs=(
            P(("tm", "seq"), None),
            P("seq", None),
            P(None, "seq"),
            P(("tm", "seq"), None),
            P(("tm", "seq"), None),
            P(),
            P(),
        ),
        out_specs=P(("tm", "seq"), None),
        check_vma=False,
    )
```

```python
import functools

import jax
import jax.numpy as jnp
from jax import lax
from jax.experimental import pallas as pl
from jax.experimental.pallas import tpu as pltpu
from jax.sharding import PartitionSpec as P

HD = 128
HEADS = 32
FRAMES = 16
BLOCK = 128
KEY_SPLIT = 4
NEG = -1e30
FLOOR = -1e29
CORES = 2
MESH = pl.DeviceIdType.MESH


def nt(a, b):
    return lax.dot_general(a, b, (((1,), (1,)), ((), ())), preferred_element_type=jnp.float32)


def tn(a, b):
    return lax.dot_general(a, b, (((0,), (0,)), ((), ())), preferred_element_type=jnp.float32)


def kernel(
    n_t, n_a, n_b,
    tok_ref, wq_ref, wo_ref, k_ref, v_ref, mask_ref, frame_ref,
    out_ref,
    bias_ref, fin, tz, tg, wq, kg, vg, wo, qp, r1, x1, r2, qs, qa, s_buf, o_s, o_g, st_s, st_g, az_s, az, ag, cs,
    tz_s, tz_r, tg_s, tg_r, tf_s, wq_s, wq_r, kg_s, kg_r, vg_s, vg_r, wo_r,
    r1_s, r1_r, r2_s, r2_r, qa_s, qa_r, os_s, os_r, ss_s, ss_r, az_ss, az_r, ag_s, ag_r, af_s, f_s, f_r,
):
    t = lax.axis_index("tm")
    s = lax.axis_index("seq")
    a = s // n_b
    b = lax.rem(s, n_b)
    n_p = n_t * n_b
    n_s = n_a * n_b
    h = t * n_b + b
    heads = qp.shape[0]
    width = heads * HD
    rows = tok_ref.shape[0]
    depth = tok_ref.shape[1] // n_a
    chunk = qp.shape[3]
    queries = n_a * chunk
    per_group = n_a // n_t
    low = lax.rem(a, 2)
    high_half = a // 2
    beside = (t, (2 * high_half + 1 - low) * n_b + b)
    across = (t, (2 * (1 - high_half) + low) * n_b + b)
    sends = []

    def plane(d):
        g = lax.rem(h + d, n_p)
        return g, g // n_b, lax.rem(g, n_b)

    core = lax.rem(b, CORES)
    mate = b - core + (CORES - 1 - core)
    n_c = n_p // CORES
    chip = h // CORES

    def same_core(d):
        g = lax.rem(chip + d, n_c) * CORES + core
        return g, g // n_b, lax.rem(g, n_b)

    def head_cols(j, g):
        return pl.ds(pl.multiple_of(g * width + j * HD, HD), HD)

    def slab(j, g):
        return ag.at[:, :, head_cols(j, g)]

    def send_weights(j):
        for db in range(1, n_b):
            b2 = lax.rem(b + db, n_b)
            send(
                wq_ref.at[:, head_cols(j, t * n_b + b2)], wq.at[j, b],
                wq_s.at[j, db], wq_r.at[j, b], (t, a * n_b + b2),
            )

    def cols(i, size):
        return pl.ds(pl.multiple_of(i * size, size), size)

    def send(src, dst, ss, rs, device):
        c = pltpu.make_async_remote_copy(
            src_ref=src, dst_ref=dst, send_sem=ss, recv_sem=rs,
            device_id=device, device_id_type=MESH,
        )
        c.start()
        sends.append(c)

    def landed(ref, sem):
        pltpu.make_async_copy(ref, ref, sem).wait()

    barrier = pltpu.get_barrier_semaphore()
    for d in range(1, n_p):
        g, t2, b2 = plane(d)
        pl.semaphore_signal(barrier, inc=1, device_id=(t2, a * n_b + b2), device_id_type=MESH)
    for da in range(1, n_a):
        for b2 in range(n_b):
            a2 = lax.rem(a + da, n_a)
            pl.semaphore_signal(barrier, inc=1, device_id=(t, a2 * n_b + b2), device_id_type=MESH)
    own = [
        pltpu.make_async_copy(tok_ref.at[:, cols(a, depth)], tz.at[a], tz_r.at[a]),
        pltpu.make_async_copy(k_ref.at[:, cols(h, width)], kg.at[h], kg_r.at[h]),
        pltpu.make_async_copy(v_ref.at[:, cols(h, width)], vg.at[h], vg_r.at[h]),
    ]
    for j in range(heads):
        own.append(pltpu.make_async_copy(
            wq_ref.at[:, head_cols(j, h)], wq.at[j, b], wq_r.at[j, b]
        ))
    for c in own:
        c.start()
    wo_copy = pltpu.make_async_copy(wo_ref, wo, wo_r)
    wo_copy.start()
    pl.semaphore_wait(barrier, n_p - 1 + (n_a - 1) * n_b)

    for da in range(1, n_a):
        a2 = lax.rem(a + da, n_a)
        send(tok_ref.at[:, cols(a2, depth)], tz.at[a], tz_s.at[da], tz_r.at[a], (t, a2 * n_b + b))
    send_weights(0)
    for i in range(n_a):
        landed(tz.at[i], tz_r.at[i])
    own_tok = pltpu.make_async_copy(tz, tg.at[t, :, b], tg_r.at[h])
    own_tok.start()
    for d in range(1, n_c):
        g, t2, b2 = same_core(d)
        send(tz, tg.at[t, :, b], tg_s.at[d], tg_r.at[h], (t2, a * n_b + b2))
    send(tz, tg.at[t, :, b], tg_s.at[0], tg_r.at[h], (t, a * n_b + mate))
    for j in range(1, heads):
        send_weights(j)
    slots = frame_ref.shape[0]
    tiles = mask_ref.shape[1]

    def allow(i, carry):
        tile = (i // n_b) * n_s + a * n_b + lax.rem(i, n_b)
        column = frame_ref[tile // tiles] * tiles + lax.rem(tile, tiles)
        for g in range(n_t):
            frame = frame_ref[g * (slots // n_t)]
            for r in range(tiles):
                lo = (g * tiles + r) * BLOCK
                value = jnp.where(mask_ref[frame, r, column] > 0, 0.0, NEG)
                bias_ref[i, :, lo:lo + BLOCK] = jnp.full((1, BLOCK), value, jnp.float32)
        return carry

    lax.fori_loop(0, n_p, allow, 0)
    for d in range(1, n_c):
        g, t2, b2 = same_core(d)
        landed(tg.at[t2, :, b2], tg_r.at[g])
        send(tg.at[t2, :, b2], tg.at[t2, :, b2], tf_s.at[d], tg_r.at[g], (t, a * n_b + mate))
    landed(tg.at[t, :, b], tg_r.at[h])
    for d in range(n_c):
        g, t2, b2 = same_core(d)
        b3 = b2 - core + (CORES - 1 - core)
        landed(tg.at[t2, :, b3], tg_r.at[t2 * n_b + b3])

    for j in range(heads):
        for i in range(n_b):
            landed(wq.at[j, i], wq_r.at[j, i])
        if j == heads - 1:
            for src, dst, ss, rs in ((k_ref, kg, kg_s, kg_r), (v_ref, vg, vg_s, vg_r)):
                for d in range(1, n_p):
                    g, t2, b2 = plane(d)
                    send(src.at[:, cols(g, width)], dst.at[h], ss.at[d], rs.at[h], (t2, a * n_b + b2))
        w_j = wq[j].reshape(depth, HD)
        for c in range(n_a):
            piece = tg.at[c // per_group][
                (c % per_group) * (n_a // per_group):(c % per_group + 1) * (n_a // per_group)
            ]
            qp[j, c // 2, c % 2] = jnp.dot(
                piece.reshape(chunk, depth), w_j, preferred_element_type=jnp.float32
            )
        send(qp.at[j, :, 1 - low], r1.at[j], r1_s.at[j], r1_r.at[j], beside)
    for j in range(heads):
        landed(r1.at[j], r1_r.at[j])
        x1[j] = qp[j, 1 - high_half, low] + r1[j, 1 - high_half]
        send(x1.at[j], r2.at[j], r2_s.at[j], r2_r.at[j], across)
    for j in range(heads):
        landed(r2.at[j], r2_r.at[j])
        total = qp[j, high_half, low] + r1[j, high_half] + r2[j]
        total = total.astype(jnp.bfloat16)
        qs[j] = total
        for da in range(1, n_a):
            a2 = lax.rem(a + da, n_a)
            send(qs.at[j], qa.at[j, a], qa_s.at[j, da], qa_r.at[j, a], (t, a2 * n_b + b))
        qa[j, a] = total

    for i in range(n_p):
        landed(kg.at[i], kg_r.at[i])

    def attend(j):
        lanes = slice(j * HD, (j + 1) * HD)
        for da in range(1, n_a):
            a2 = lax.rem(a + da, n_a)
            landed(qa.at[j, a2], qa_r.at[j, a2])
        q_j = qa[j].reshape(queries, HD)

        def score(i, high):
            sc = nt(kg[i, :, lanes], q_j) * (HD ** -0.5) + bias_ref[i]
            s_buf[i] = sc
            return jnp.maximum(high, jnp.max(sc, axis=0, keepdims=True))

        high = lax.fori_loop(
            0, n_p, score, jnp.full((1, queries), FLOOR, jnp.float32), unroll=2
        )
        if j == 0:
            for i in range(n_p):
                landed(vg.at[i], vg_r.at[i])

        def mix(i, state):
            denom, acc = state
            w = jnp.exp(s_buf[i] - high)
            return (
                denom + jnp.sum(w, axis=0, keepdims=True),
                acc + tn(vg[i, :, lanes], w.astype(jnp.bfloat16)),
            )

        denom, acc = lax.fori_loop(
            0, n_p, mix,
            (jnp.zeros((1, queries), jnp.float32), jnp.zeros((HD, queries), jnp.float32)),
            unroll=2,
        )
        out = (acc / jnp.where(denom > 0.0, denom, 1.0)).astype(jnp.bfloat16)
        for c in range(n_a):
            lo = c * chunk
            o_s[j, c] = out[:, lo:lo + chunk]
            st_s[j, c, 0:1] = high[:, lo:lo + chunk]
            st_s[j, c, 1:2] = denom[:, lo:lo + chunk]
            st_s[j, c, 2:8] = jnp.zeros((6, chunk), jnp.float32)
        for da in range(1, n_a):
            a2 = lax.rem(a + da, n_a)
            there = (t, a2 * n_b + b)
            send(o_s.at[j, a2], o_g.at[j, a], os_s.at[j, da], os_r.at[j, a], there)
            send(st_s.at[j, a2], st_g.at[j, a], ss_s.at[j, da], ss_r.at[j, a], there)
        o_g[j, a] = o_s[j, a]
        st_g[j, a] = st_s[j, a]

    def combine(j):
        for da in range(1, n_a):
            a2 = lax.rem(a + da, n_a)
            landed(o_g.at[j, a2], os_r.at[j, a2])
            landed(st_g.at[j, a2], ss_r.at[j, a2])
        high = st_g[j, 0, 0:1]
        for i in range(1, n_a):
            high = jnp.maximum(high, st_g[j, i, 0:1])
        den = jnp.zeros((1, chunk), jnp.float32)
        num = jnp.zeros((HD, chunk), jnp.float32)
        for i in range(n_a):
            w = st_g[j, i, 1:2] * jnp.exp(st_g[j, i, 0:1] - high)
            den = den + w
            num = num + w * o_g[j, i].astype(jnp.float32)
        res = jnp.transpose(num / den).astype(jnp.bfloat16)
        az_s[j] = res
        send(az_s.at[j], az.at[j, a], az_ss.at[j, 0], az_r.at[j, a], across)
        send(az_s.at[j], az.at[j, a], az_ss.at[j, 1], az_r.at[j, a], beside)
        az[j, a] = res

    def relay(j):
        far = 2 * (1 - high_half) + low
        landed(az.at[j, far], az_r.at[j, far])
        send(az.at[j, far], az.at[j, far], az_ss.at[j, 2], az_r.at[j, far], beside)

    def spread(j):
        for half in range(2):
            other = 2 * half + 1 - low
            landed(az.at[j, other], az_r.at[j, other])
        for d in range(n_c):
            g, t2, b2 = same_core(d)
            send(
                az.at[j, pl.ds(t2 * per_group, per_group)], slab(j, h),
                ag_s.at[j, d], ag_r.at[j, h], (t2, a * n_b + (b2 if d else mate)),
            )
        at = pl.multiple_of(h * width + j * HD, HD)
        ag[:, :, pl.ds(at, HD)] = az[j, pl.ds(t * per_group, per_group)]

    def forward(j):
        for d in range(1, n_c):
            g, t2, b2 = same_core(d)
            landed(slab(j, g), ag_r.at[j, g])
            send(slab(j, g), slab(j, g), af_s.at[j, d], ag_r.at[j, g], (t, a * n_b + mate))

    stages = (attend, combine, relay, spread, forward)
    for step in range(heads + len(stages) - 1):
        order = range(len(stages)) if step < heads else reversed(range(len(stages)))
        for lag in order:
            if 0 <= step - lag < heads:
                stages[lag](step - lag)

    wo_copy.wait()
    group_rows = per_group * chunk
    for j in range(heads):
        for d in range(n_c):
            g, t2, b2 = same_core(d)
            g3 = g - core + (CORES - 1 - core)
            landed(slab(j, g3), ag_r.at[j, g3])
    total = nt(ag[...].reshape(group_rows, n_p * width), wo[...])
    cs[...] = total.astype(jnp.bfloat16).reshape(cs.shape)
    for d in range(1, n_s):
        s2 = lax.rem(s + d, n_s)
        send(cs.at[s2], fin.at[s], f_s.at[d], f_r.at[s], (t, s2))
    fin[s] = cs[s]
    for d in range(1, n_s):
        s2 = lax.rem(s + d, n_s)
        landed(fin.at[s2], f_r.at[s2])
    wide = fin.shape[2]
    for i in range(n_s):
        out_ref[:, i * wide:(i + 1) * wide] = fin[i]
    for c in sends:
        c.wait_send()


def on_device(tokens, w_query, w_out, k_cache, v_cache, radial_mask, slot_frame):
    n_s = lax.axis_size("seq")
    n_t = lax.axis_size("tm")
    n_a = KEY_SPLIT
    n_b = n_s // n_a
    n_p = n_t * n_b
    heads = HEADS // n_p
    width = heads * HD
    rows, d_model = tokens.shape
    depth = d_model // n_a
    queries = n_t * n_s * rows
    chunk = queries // n_a
    per_group = n_a // n_t
    keys = k_cache.shape[0]
    w_rows = w_query.shape[0]
    out_cols = w_out.shape[1]

    bf, f32 = jnp.bfloat16, jnp.float32
    vm, dma = pltpu.VMEM, pltpu.SemaphoreType.DMA
    hbm = pl.BlockSpec(memory_space=pl.ANY)
    vmem = pl.BlockSpec(memory_space=pltpu.VMEM)
    smem = pl.BlockSpec(memory_space=pltpu.SMEM)
    return pl.pallas_call(
        functools.partial(kernel, n_t, n_a, n_b),
        out_shape=jax.ShapeDtypeStruct((rows, n_s * out_cols), bf),
        in_specs=[hbm] * 5 + [smem] * 2,
        out_specs=vmem,
        scratch_shapes=[
            vm((n_p, 1, queries), f32),
            vm((n_s, rows, out_cols), bf),
            vm((n_a, rows, depth), bf),
            vm((n_t, n_a, n_b, rows, depth), bf),
            vm((heads, n_b, w_rows, HD), bf),
            vm((n_p, keys, width), bf),
            vm((n_p, keys, width), bf),
            vm(w_out.shape[::-1], bf),
            vm((heads, 2, 2, chunk, HD), f32),
            vm((heads, 2, chunk, HD), f32),
            vm((heads, chunk, HD), f32),
            vm((heads, chunk, HD), f32),
            vm((heads, chunk, HD), bf),
            vm((heads, n_a, chunk, HD), bf),
            vm((n_p, keys, queries), f32),
            vm((heads, n_a, HD, chunk), bf),
            vm((heads, n_a, HD, chunk), bf),
            vm((heads, n_a, 8, chunk), f32),
            vm((heads, n_a, 8, chunk), f32),
            vm((heads, chunk, HD), bf),
            vm((heads, n_a, chunk, HD), bf),
            vm((per_group, chunk, n_p * width), bf),
            vm((n_s, rows, out_cols), bf),
            dma((n_a,)), dma((n_a,)),
            dma((n_p,)), dma((n_p,)), dma((n_p,)),
            dma((heads, n_b)), dma((heads, n_b)),
            dma((n_p,)), dma((n_p,)),
            dma((n_p,)), dma((n_p,)),
            dma,
            dma((heads,)), dma((heads,)), dma((heads,)), dma((heads,)),
            dma((heads, n_a)), dma((heads, n_a)),
            dma((heads, n_a)), dma((heads, n_a)),
            dma((heads, n_a)), dma((heads, n_a)),
            dma((heads, n_a)), dma((heads, n_a)),
            dma((heads, n_p)), dma((heads, n_p)), dma((heads, n_p)),
            dma((n_s,)), dma((n_s,)),
        ],
        compiler_params=pltpu.CompilerParams(
            collective_id=0, has_side_effects=True, vmem_limit_bytes=60 * 1024 * 1024
        ),
    )(tokens, w_query, w_out.T, k_cache, v_cache, radial_mask, slot_frame)


def solution(mesh):
    return jax.shard_map(
        on_device,
        mesh=mesh,
        in_specs=(
            P(("tm", "seq"), None),
            P("seq", None),
            P(None, "seq"),
            P(("tm", "seq"), None),
            P(("tm", "seq"), None),
            P(),
            P(),
        ),
        out_specs=P(("tm", "seq"), None),
        check_vma=False,
    )
```

```python
import functools

import jax
import jax.numpy as jnp
from jax import lax
from jax.experimental import pallas as pl
from jax.experimental.pallas import tpu as pltpu
from jax.sharding import PartitionSpec as P

HD = 128
HEADS = 32
FRAMES = 16
BLOCK = 128
KEY_SPLIT = 4
NEG = -1e30
FLOOR = -1e29
CORES = 2
MESH = pl.DeviceIdType.MESH


def nt(a, b):
    return lax.dot_general(a, b, (((1,), (1,)), ((), ())), preferred_element_type=jnp.float32)


def tn(a, b):
    return lax.dot_general(a, b, (((0,), (0,)), ((), ())), preferred_element_type=jnp.float32)


def kernel(
    n_t, n_a, n_b,
    tok_ref, wq_ref, wo_ref, k_ref, v_ref, mask_ref, frame_ref,
    out_ref,
    bias_ref, fin, tz, tg, wq, kg, vg, wo, qp, r1, x1, r2, qs, qa, s_buf, o_s, o_g, st_s, st_g, az_s, az, ag, cs,
    tz_s, tz_r, tg_s, tg_r, tf_s, wq_s, wq_r, kg_s, kg_r, vg_s, vg_r, wo_r,
    r1_s, r1_r, r2_s, r2_r, qa_s, qa_r, os_s, os_r, ss_s, ss_r, az_ss, az_r, ag_s, ag_r, af_s, f_s, f_r,
):
    t = lax.axis_index("tm")
    s = lax.axis_index("seq")
    a = s // n_b
    b = lax.rem(s, n_b)
    n_p = n_t * n_b
    n_s = n_a * n_b
    h = t * n_b + b
    heads = qp.shape[0]
    width = heads * HD
    rows = tok_ref.shape[0]
    depth = tok_ref.shape[1] // n_a
    chunk = qp.shape[3]
    queries = n_a * chunk
    per_group = n_a // n_t
    low = lax.rem(a, 2)
    high_half = a // 2
    beside = (t, (2 * high_half + 1 - low) * n_b + b)
    across = (t, (2 * (1 - high_half) + low) * n_b + b)
    sends = []

    def plane(d):
        g = lax.rem(h + d, n_p)
        return g, g // n_b, lax.rem(g, n_b)

    core = lax.rem(b, CORES)
    mate = b - core + (CORES - 1 - core)
    n_c = n_p // CORES
    chip = h // CORES

    def same_core(d):
        g = lax.rem(chip + d, n_c) * CORES + core
        return g, g // n_b, lax.rem(g, n_b)

    def head_cols(j, g):
        return pl.ds(pl.multiple_of(g * width + j * HD, HD), HD)

    def slab(j, g):
        return ag.at[:, :, head_cols(j, g)]

    def send_weights(j):
        for db in range(1, n_b):
            b2 = lax.rem(b + db, n_b)
            send(
                wq_ref.at[:, head_cols(j, t * n_b + b2)], wq.at[j, b],
                wq_s.at[j, db], wq_r.at[j, b], (t, a * n_b + b2),
            )

    def cols(i, size):
        return pl.ds(pl.multiple_of(i * size, size), size)

    def send(src, dst, ss, rs, device):
        c = pltpu.make_async_remote_copy(
            src_ref=src, dst_ref=dst, send_sem=ss, recv_sem=rs,
            device_id=device, device_id_type=MESH,
        )
        c.start()
        sends.append(c)

    def landed(ref, sem):
        pltpu.make_async_copy(ref, ref, sem).wait()

    barrier = pltpu.get_barrier_semaphore()
    for d in range(1, n_p):
        g, t2, b2 = plane(d)
        pl.semaphore_signal(barrier, inc=1, device_id=(t2, a * n_b + b2), device_id_type=MESH)
    for da in range(1, n_a):
        for b2 in range(n_b):
            a2 = lax.rem(a + da, n_a)
            pl.semaphore_signal(barrier, inc=1, device_id=(t, a2 * n_b + b2), device_id_type=MESH)
    own = [
        pltpu.make_async_copy(tok_ref.at[:, cols(a, depth)], tz.at[a], tz_r.at[a]),
    ]
    for j in range(heads):
        own.append(pltpu.make_async_copy(
            wq_ref.at[:, head_cols(j, h)], wq.at[j, b], wq_r.at[j, b]
        ))
        own.append(pltpu.make_async_copy(
            k_ref.at[:, head_cols(j, h)], kg.at[j, h], kg_r.at[j, h]
        ))
        own.append(pltpu.make_async_copy(
            v_ref.at[:, head_cols(j, h)], vg.at[j, h], vg_r.at[j, h]
        ))
    for c in own:
        c.start()
    wo_copy = pltpu.make_async_copy(wo_ref, wo, wo_r)
    wo_copy.start()
    pl.semaphore_wait(barrier, n_p - 1 + (n_a - 1) * n_b)

    for da in range(1, n_a):
        a2 = lax.rem(a + da, n_a)
        send(tok_ref.at[:, cols(a2, depth)], tz.at[a], tz_s.at[da], tz_r.at[a], (t, a2 * n_b + b))
    send_weights(0)
    for i in range(n_a):
        landed(tz.at[i], tz_r.at[i])
    own_tok = pltpu.make_async_copy(tz, tg.at[t, :, b], tg_r.at[h])
    own_tok.start()
    for d in range(1, n_c):
        g, t2, b2 = same_core(d)
        send(tz, tg.at[t, :, b], tg_s.at[d], tg_r.at[h], (t2, a * n_b + b2))
    send(tz, tg.at[t, :, b], tg_s.at[0], tg_r.at[h], (t, a * n_b + mate))
    for j in range(1, heads):
        send_weights(j)
    slots = frame_ref.shape[0]
    tiles = mask_ref.shape[1]

    def allow(i, carry):
        tile = (i // n_b) * n_s + a * n_b + lax.rem(i, n_b)
        column = frame_ref[tile // tiles] * tiles + lax.rem(tile, tiles)
        for g in range(n_t):
            frame = frame_ref[g * (slots // n_t)]
            for r in range(tiles):
                lo = (g * tiles + r) * BLOCK
                value = jnp.where(mask_ref[frame, r, column] > 0, 0.0, NEG)
                bias_ref[i, :, lo:lo + BLOCK] = jnp.full((1, BLOCK), value, jnp.float32)
        return carry

    lax.fori_loop(0, n_p, allow, 0)
    for d in range(1, n_c):
        g, t2, b2 = same_core(d)
        landed(tg.at[t2, :, b2], tg_r.at[g])
        send(tg.at[t2, :, b2], tg.at[t2, :, b2], tf_s.at[d], tg_r.at[g], (t, a * n_b + mate))
    landed(tg.at[t, :, b], tg_r.at[h])
    for d in range(n_c):
        g, t2, b2 = same_core(d)
        b3 = b2 - core + (CORES - 1 - core)
        landed(tg.at[t2, :, b3], tg_r.at[t2 * n_b + b3])

    for j in range(heads):
        for i in range(n_b):
            landed(wq.at[j, i], wq_r.at[j, i])
        if j == heads - 1:
            for i in range(heads):
                for src, dst, ss, rs in ((k_ref, kg, kg_s, kg_r), (v_ref, vg, vg_s, vg_r)):
                    for d in range(1, n_p):
                        g, t2, b2 = plane(d)
                        send(
                            src.at[:, head_cols(i, g)], dst.at[i, h],
                            ss.at[i, d], rs.at[i, h], (t2, a * n_b + b2),
                        )
        w_j = wq[j].reshape(depth, HD)
        for c in range(n_a):
            piece = tg.at[c // per_group][
                (c % per_group) * (n_a // per_group):(c % per_group + 1) * (n_a // per_group)
            ]
            qp[j, c // 2, c % 2] = jnp.dot(
                piece.reshape(chunk, depth), w_j, preferred_element_type=jnp.float32
            )
        send(qp.at[j, :, 1 - low], r1.at[j], r1_s.at[j], r1_r.at[j], beside)

    def reduce_pair(j):
        landed(r1.at[j], r1_r.at[j])
        x1[j] = qp[j, 1 - high_half, low] + r1[j, 1 - high_half]
        send(x1.at[j], r2.at[j], r2_s.at[j], r2_r.at[j], across)

    def reduce_across(j):
        landed(r2.at[j], r2_r.at[j])
        total = qp[j, high_half, low] + r1[j, high_half] + r2[j]
        total = total.astype(jnp.bfloat16)
        qs[j] = total
        for da in range(1, n_a):
            a2 = lax.rem(a + da, n_a)
            send(qs.at[j], qa.at[j, a], qa_s.at[j, da], qa_r.at[j, a], (t, a2 * n_b + b))
        qa[j, a] = total

    def attend(j):
        for da in range(1, n_a):
            a2 = lax.rem(a + da, n_a)
            landed(qa.at[j, a2], qa_r.at[j, a2])
        q_j = qa[j].reshape(queries, HD)

        for i in range(n_p):
            landed(kg.at[j, i], kg_r.at[j, i])

        def score(i, high):
            sc = nt(kg[j, i], q_j) * (HD ** -0.5) + bias_ref[i]
            s_buf[i] = sc
            return jnp.maximum(high, jnp.max(sc, axis=0, keepdims=True))

        high = lax.fori_loop(
            0, n_p, score, jnp.full((1, queries), FLOOR, jnp.float32), unroll=2
        )
        for i in range(n_p):
            landed(vg.at[j, i], vg_r.at[j, i])

        def mix(i, state):
            denom, acc = state
            w = jnp.exp(s_buf[i] - high)
            return (
                denom + jnp.sum(w, axis=0, keepdims=True),
                acc + tn(vg[j, i], w.astype(jnp.bfloat16)),
            )

        denom, acc = lax.fori_loop(
            0, n_p, mix,
            (jnp.zeros((1, queries), jnp.float32), jnp.zeros((HD, queries), jnp.float32)),
            unroll=2,
        )
        out = (acc / jnp.where(denom > 0.0, denom, 1.0)).astype(jnp.bfloat16)
        for c in range(n_a):
            lo = c * chunk
            o_s[j, c] = out[:, lo:lo + chunk]
            st_s[j, c, 0:1] = high[:, lo:lo + chunk]
            st_s[j, c, 1:2] = denom[:, lo:lo + chunk]
            st_s[j, c, 2:8] = jnp.zeros((6, chunk), jnp.float32)
        for da in range(1, n_a):
            a2 = lax.rem(a + da, n_a)
            there = (t, a2 * n_b + b)
            send(o_s.at[j, a2], o_g.at[j, a], os_s.at[j, da], os_r.at[j, a], there)
            send(st_s.at[j, a2], st_g.at[j, a], ss_s.at[j, da], ss_r.at[j, a], there)
        o_g[j, a] = o_s[j, a]
        st_g[j, a] = st_s[j, a]

    def combine(j):
        for da in range(1, n_a):
            a2 = lax.rem(a + da, n_a)
            landed(o_g.at[j, a2], os_r.at[j, a2])
            landed(st_g.at[j, a2], ss_r.at[j, a2])
        high = st_g[j, 0, 0:1]
        for i in range(1, n_a):
            high = jnp.maximum(high, st_g[j, i, 0:1])
        den = jnp.zeros((1, chunk), jnp.float32)
        num = jnp.zeros((HD, chunk), jnp.float32)
        for i in range(n_a):
            w = st_g[j, i, 1:2] * jnp.exp(st_g[j, i, 0:1] - high)
            den = den + w
            num = num + w * o_g[j, i].astype(jnp.float32)
        res = jnp.transpose(num / den).astype(jnp.bfloat16)
        az_s[j] = res
        send(az_s.at[j], az.at[j, a], az_ss.at[j, 0], az_r.at[j, a], across)
        send(az_s.at[j], az.at[j, a], az_ss.at[j, 1], az_r.at[j, a], beside)
        az[j, a] = res

    def relay(j):
        far = 2 * (1 - high_half) + low
        landed(az.at[j, far], az_r.at[j, far])
        send(az.at[j, far], az.at[j, far], az_ss.at[j, 2], az_r.at[j, far], beside)

    def spread(j):
        for half in range(2):
            other = 2 * half + 1 - low
            landed(az.at[j, other], az_r.at[j, other])
        for d in range(n_c):
            g, t2, b2 = same_core(d)
            send(
                az.at[j, pl.ds(t2 * per_group, per_group)], slab(j, h),
                ag_s.at[j, d], ag_r.at[j, h], (t2, a * n_b + (b2 if d else mate)),
            )
        at = pl.multiple_of(h * width + j * HD, HD)
        ag[:, :, pl.ds(at, HD)] = az[j, pl.ds(t * per_group, per_group)]

    def forward(j):
        for d in range(1, n_c):
            g, t2, b2 = same_core(d)
            landed(slab(j, g), ag_r.at[j, g])
            send(slab(j, g), slab(j, g), af_s.at[j, d], ag_r.at[j, g], (t, a * n_b + mate))

    stages = (reduce_pair, reduce_across, attend, combine, relay, spread, forward)
    for step in range(heads + len(stages) - 1):
        order = range(len(stages)) if step < heads + 2 else reversed(range(len(stages)))
        for lag in order:
            if 0 <= step - lag < heads:
                stages[lag](step - lag)

    wo_copy.wait()
    group_rows = per_group * chunk
    for j in range(heads):
        for d in range(n_c):
            g, t2, b2 = same_core(d)
            g3 = g - core + (CORES - 1 - core)
            landed(slab(j, g3), ag_r.at[j, g3])
    total = nt(ag[...].reshape(group_rows, n_p * width), wo[...])
    cs[...] = total.astype(jnp.bfloat16).reshape(cs.shape)
    for d in range(1, n_s):
        s2 = lax.rem(s + d, n_s)
        send(cs.at[s2], fin.at[s], f_s.at[d], f_r.at[s], (t, s2))
    fin[s] = cs[s]
    for d in range(1, n_s):
        s2 = lax.rem(s + d, n_s)
        landed(fin.at[s2], f_r.at[s2])
    wide = fin.shape[2]
    for i in range(n_s):
        out_ref[:, i * wide:(i + 1) * wide] = fin[i]
    for c in sends:
        c.wait_send()


def on_device(tokens, w_query, w_out, k_cache, v_cache, radial_mask, slot_frame):
    n_s = lax.axis_size("seq")
    n_t = lax.axis_size("tm")
    n_a = KEY_SPLIT
    n_b = n_s // n_a
    n_p = n_t * n_b
    heads = HEADS // n_p
    width = heads * HD
    rows, d_model = tokens.shape
    depth = d_model // n_a
    queries = n_t * n_s * rows
    chunk = queries // n_a
    per_group = n_a // n_t
    keys = k_cache.shape[0]
    w_rows = w_query.shape[0]
    out_cols = w_out.shape[1]

    bf, f32 = jnp.bfloat16, jnp.float32
    vm, dma = pltpu.VMEM, pltpu.SemaphoreType.DMA
    hbm = pl.BlockSpec(memory_space=pl.ANY)
    vmem = pl.BlockSpec(memory_space=pltpu.VMEM)
    smem = pl.BlockSpec(memory_space=pltpu.SMEM)
    return pl.pallas_call(
        functools.partial(kernel, n_t, n_a, n_b),
        out_shape=jax.ShapeDtypeStruct((rows, n_s * out_cols), bf),
        in_specs=[hbm] * 5 + [smem] * 2,
        out_specs=vmem,
        scratch_shapes=[
            vm((n_p, 1, queries), f32),
            vm((n_s, rows, out_cols), bf),
            vm((n_a, rows, depth), bf),
            vm((n_t, n_a, n_b, rows, depth), bf),
            vm((heads, n_b, w_rows, HD), bf),
            vm((heads, n_p, keys, HD), bf),
            vm((heads, n_p, keys, HD), bf),
            vm(w_out.shape[::-1], bf),
            vm((heads, 2, 2, chunk, HD), f32),
            vm((heads, 2, chunk, HD), f32),
            vm((heads, chunk, HD), f32),
            vm((heads, chunk, HD), f32),
            vm((heads, chunk, HD), bf),
            vm((heads, n_a, chunk, HD), bf),
            vm((n_p, keys, queries), f32),
            vm((heads, n_a, HD, chunk), bf),
            vm((heads, n_a, HD, chunk), bf),
            vm((heads, n_a, 8, chunk), f32),
            vm((heads, n_a, 8, chunk), f32),
            vm((heads, chunk, HD), bf),
            vm((heads, n_a, chunk, HD), bf),
            vm((per_group, chunk, n_p * width), bf),
            vm((n_s, rows, out_cols), bf),
            dma((n_a,)), dma((n_a,)),
            dma((n_p,)), dma((n_p,)), dma((n_p,)),
            dma((heads, n_b)), dma((heads, n_b)),
            dma((heads, n_p)), dma((heads, n_p)),
            dma((heads, n_p)), dma((heads, n_p)),
            dma,
            dma((heads,)), dma((heads,)), dma((heads,)), dma((heads,)),
            dma((heads, n_a)), dma((heads, n_a)),
            dma((heads, n_a)), dma((heads, n_a)),
            dma((heads, n_a)), dma((heads, n_a)),
            dma((heads, n_a)), dma((heads, n_a)),
            dma((heads, n_p)), dma((heads, n_p)), dma((heads, n_p)),
            dma((n_s,)), dma((n_s,)),
        ],
        compiler_params=pltpu.CompilerParams(
            collective_id=0, has_side_effects=True, vmem_limit_bytes=60 * 1024 * 1024
        ),
    )(tokens, w_query, w_out.T, k_cache, v_cache, radial_mask, slot_frame)


def solution(mesh):
    return jax.shard_map(
        on_device,
        mesh=mesh,
        in_specs=(
            P(("tm", "seq"), None),
            P("seq", None),
            P(None, "seq"),
            P(("tm", "seq"), None),
            P(("tm", "seq"), None),
            P(),
            P(),
        ),
        out_specs=P(("tm", "seq"), None),
        check_vma=False,
    )
```
